32 devices in a mesh: blk: 8 (over z, y), col: 4 (over x, core).
Axes of the slice: x: 2, y: 2, z: 4, core: 2. Of those that a mesh axis runs over, the one named last changes fastest.
Arguments:
- amplitudes: float32 [800, 32, 1601], P('col', 'blk'), may hold values from -6 to 6
- integrals: float32 [2, 1024, 20, 1601], P(None, 'blk', 'col'), may hold values from -0.03125 to 0.03125
- block_ids: int32 [20], replicated, may hold values from 0 to 799, as said below
- mirror: int32 [16], replicated, may hold values from 0 to 15, each once
Outputs:
- ladder_residual: float32 [16, 1024], P('col', 'blk')
The draws below stay inside these ranges and needn't reach their ends.
Inputs may be any that keep to these rules, and one draw needn't show every extreme that they name: `block_ids`: 20 distinct folded block numbers; 0 and 799 are always among them. `mirror`: a permutation of the slab positions.
All inputs are finite; a program needn't handle non-finite values.
Results may differ from the reference program's by a relative error of at most 0.000073.
Values sent between devices are 32-bit elements; how exact they have to be, the bound alone decides.
A program may use at most 64 MiB of HBM per device.

```python
import jax
import jax.numpy as jnp
from jax import lax

NPAIR = 16
L = 1601
H = 800
AB = 1024
NB = 20


def draw_block_ids(key, part):
    inner = jax.random.permutation(key, H - 2)[:NB - 2] + 1
    chosen = jnp.concatenate([jnp.array([0, H - 1], jnp.int32), inner.astype(jnp.int32)])
    shuffle = jax.random.permutation(jax.random.fold_in(key, 7), NB)
    return chosen[shuffle]


def shard_levels(own_key, dims, split, low, high):
    def one(position, blocks):
        heights = jax.random.uniform(jax.random.fold_in(jax.random.fold_in(own_key, 6), position), (blocks,), jnp.float32, low / len(split), high / len(split))
        return jnp.repeat(jnp.exp(heights), dims[position] // blocks).reshape((-1,) + (1,) * (len(dims) - position - 1))

    gain = one(*split[0])
    for cut in split[1:]:
        gain = gain * one(*cut)
    return gain


def scatter_about(stream_key, dims, deviation, bound, cuts=(), held_as=jnp.bfloat16):
    loudness = shard_levels(stream_key, dims, cuts, -0.22, 0.18) if cuts else 1.0
    entries = jax.random.normal(stream_key, dims, jnp.float32) * deviation * loudness
    return jnp.minimum(jnp.maximum(entries, -bound), bound).astype(held_as)


def setup_inputs(seed: int = 0) -> dict:
    arg_keys = jax.random.split(jax.random.key(seed), 5)
    amplitudes = scatter_about(arg_keys[0], (H, 2 * NPAIR, L), 1.0, 6.0, ((0, 4), (1, 8)), jnp.float32)
    integrals = scatter_about(arg_keys[1], (2, AB, NB, L), (NB * L) ** -0.5, 0.03125, ((1, 8), (2, 4)), jnp.float32)
    block_ids = draw_block_ids(jax.random.fold_in(arg_keys[4], 71), 0)
    mirror = jax.random.permutation(arg_keys[3], NPAIR).astype(jnp.int32)
    return {"amplitudes": amplitudes, "integrals": integrals, "block_ids": block_ids, "mirror": mirror}


def reference(amplitudes, integrals, block_ids, mirror):
    selected = jnp.take(amplitudes, block_ids, axis=0)
    plus_part = jnp.einsum("krl,akl->ra", selected, integrals[0], precision=lax.Precision.HIGHEST)
    minus_part = jnp.einsum("krl,akl->ra", selected, integrals[1], precision=lax.Precision.HIGHEST)
    pair_count = plus_part.shape[0] // 2
    direct = 0.5 * (plus_part[:pair_count] + minus_part[:pair_count] + plus_part[pair_count:] - minus_part[pair_count:])
    swapped = 0.5 * (plus_part[:pair_count] - minus_part[:pair_count] + plus_part[pair_count:] + minus_part[pair_count:])
    return direct + jnp.take(swapped, mirror, axis=0)
```

```python
import functools

import jax
import jax.numpy as jnp
from jax import lax
from jax.experimental import pallas as pl
from jax.experimental.pallas import tpu as pltpu
from jax.sharding import PartitionSpec as P

MESH = pl.DeviceIdType.MESH


def kernel(
    nblk, ncol,
    amp_hbm, int_hbm, ids, mirror, out_ref,
    amp_v, int_v, hi, lo, sendb, landed, gath, feed, swp, osend, orecv,
    amp_sem, int_sem, xs, xr, us, ds, ys, gr, os_, or_,
):
    blocks_here = amp_v.shape[0]
    own = int_v.shape[0]
    rows = amp_v.shape[1]
    width = amp_v.shape[2]
    ab = int_v.shape[2]
    padded = hi.shape[1]
    pairs = feed.shape[0] // 2
    own_pairs = osend.shape[1]
    nhi = nblk // 2
    half = nblk // 2
    b = lax.axis_index("blk")
    c = lax.axis_index("col")
    z = b // 2
    y = b % 2
    partner = z * 2 + (1 - y)

    amp_copy = pltpu.make_async_copy(amp_hbm, amp_v, amp_sem)
    amp_copy.start()
    int_copies = {}
    for k in range(own):
        cp = pltpu.make_async_copy(int_hbm.at[k], int_v.at[k].reshape(width, 2, ab), int_sem.at[k])
        cp.start()
        int_copies[k] = cp

    barrier = pltpu.get_barrier_semaphore()
    for j in range(1, ncol):
        pl.semaphore_signal(barrier, inc=1, device_id=(b, (c + j) % ncol), device_id_type=MESH)
    pl.semaphore_signal(barrier, inc=1, device_id=(partner, c), device_id_type=MESH)

    @pl.when(z < nhi - 1)
    def _():
        pl.semaphore_signal(barrier, inc=1, device_id=(b + 2, c), device_id_type=MESH)

    @pl.when(z > 0)
    def _():
        pl.semaphore_signal(barrier, inc=1, device_id=(b - 2, c), device_id_type=MESH)

    ends = (z == 0).astype(jnp.int32) + (z == nhi - 1).astype(jnp.int32)
    pl.semaphore_wait(barrier, ncol + 2 - ends)

    def xcopy(k, j):
        return pltpu.make_async_remote_copy(
            src_ref=sendb.at[j, k], dst_ref=landed.at[j, k],
            send_sem=xs.at[j, k], recv_sem=xr.at[j, k],
            device_id=(b, (c + j) % ncol), device_id_type=MESH)

    def gcopy(k, src, sem, target):
        return pltpu.make_async_remote_copy(
            src_ref=gath.at[k, src], dst_ref=gath.at[k, src],
            send_sem=sem, recv_sem=gr.at[k, src],
            device_id=(target, c), device_id_type=MESH)

    def up(k, d):
        return gcopy(k, b - 2 * d, us.at[k, d], b + 2)

    def down(k, d):
        return gcopy(k, b + 2 * d, ds.at[k, d], b - 2)

    def across(k, zz):
        return gcopy(k, zz * 2 + y, ys.at[k, zz], partner)

    def arrived(k, src):
        gcopy(k, src, us.at[k, 0], partner).wait_recv()

    base = c * blocks_here

    def wanted(k, dest):
        here = ids[dest * own + k] - base
        ok = jnp.logical_and(here >= 0, here < blocks_here)
        at = jnp.minimum(jnp.maximum(here, 0), blocks_here - 1)
        return jnp.where(ok, amp_v[at], 0.0)

    amp_copy.wait()
    for k in range(own):
        for j in range(1, ncol):
            sendb[j, k] = wanted(k, (c + j) % ncol)
            xcopy(k, j).start()
    for k in range(own):
        sendb[0, k] = wanted(k, c)

    tail = (width // 128) * 128
    if padded > width:
        feed[:, tail:] = jnp.zeros((2 * pairs, padded - tail), jnp.float32)

    def convert(k):
        int_copies[k].wait()
        whole = width // 16

        def split(at, count):
            for w in range(2):
                v = int_v[k, pl.ds(at * 2 + w, count, stride=2), :]
                h = v.astype(jnp.bfloat16)
                l = (v - h.astype(jnp.float32)).astype(jnp.bfloat16)
                if count < 16:
                    blank = jnp.zeros((16 - count, ab), jnp.bfloat16)
                    h = jnp.concatenate([h, blank], axis=0)
                    l = jnp.concatenate([l, blank], axis=0)
                hi[k, pl.ds(at, 16), w * ab:(w + 1) * ab] = h
                lo[k, pl.ds(at, 16), w * ab:(w + 1) * ab] = l

        def strip(i, carry):
            split(pl.multiple_of(i * 16, 16), 16)
            return carry

        lax.fori_loop(0, whole, strip, 0, unroll=4)
        end = whole * 16
        if width > end:
            split(end, width - end)
            end += 16
        if padded > end:
            hi[k, end:] = jnp.zeros((padded - end, 2 * ab), jnp.bfloat16)
            lo[k, end:] = jnp.zeros((padded - end, 2 * ab), jnp.bfloat16)

    def own_piece(k):
        for j in range(1, ncol):
            xcopy(k, j).wait_recv()
        total = sendb[0, k]
        for j in range(1, ncol):
            total = total + landed[j, k]
        gath[k, b] = total
        across(k, z).start()

        @pl.when(z < nhi - 1)
        def _():
            up(k, 0).start()

        @pl.when(z > 0)
        def _():
            down(k, 0).start()

    def relay(k, d):
        @pl.when(z >= d)
        def _():
            arrived(k, b - 2 * d)

            @pl.when(z < nhi - 1)
            def _():
                up(k, d).start()

            across(k, z - d).start()

        @pl.when(z + d < nhi)
        def _():
            arrived(k, b + 2 * d)

            @pl.when(z > 0)
            def _():
                down(k, d).start()

            across(k, z + d).start()

    def multiply(k, acc):
        for zz in range(nhi):
            arrived(k, zz * 2 + 1 - y)
        for i in range(half):
            first = gath[k, i]
            second = gath[k, half + i]
            feed[i * rows:(i + 1) * rows, :width] = first + second
            feed[pairs + i * rows:pairs + (i + 1) * rows, :width] = first - second
        f = feed[...]
        fh = f.astype(jnp.bfloat16)
        fl = (f - fh.astype(jnp.float32)).astype(jnp.bfloat16)
        both = jnp.concatenate([fh, fl], axis=0)
        big = jnp.dot(both, hi[k], preferred_element_type=jnp.float32)
        small = jnp.dot(fh, lo[k], preferred_element_type=jnp.float32)
        part = big[:2 * pairs] + (big[2 * pairs:] + small)
        new = [part[:pairs, :ab], part[pairs:, ab:]]
        return new if acc is None else [u + v for u, v in zip(acc, new)]

    convert(0)
    for t in range(own + nhi - 1):
        if t < own:
            own_piece(t)
            if t + 1 < own:
                convert(t + 1)
        for d in range(1, nhi):
            k = t - d
            if 0 <= k < own:
                relay(k, d)
    acc = None
    for k in range(own):
        acc = multiply(k, acc)

    x_part, y_part = acc
    swp[...] = 0.5 * (x_part - y_part)
    direct = 0.5 * (x_part + y_part)
    for q in range(ncol):
        for i in range(own_pairs):
            p = q * own_pairs + i
            osend[q, i:i + 1, :] = direct[p:p + 1] + swp[pl.ds(mirror[p], 1), :]

    def ocopy(j):
        dest = (c + j) % ncol
        return pltpu.make_async_remote_copy(
            src_ref=osend.at[dest], dst_ref=orecv.at[j],
            send_sem=os_.at[j], recv_sem=or_.at[j],
            device_id=(b, dest), device_id_type=MESH)

    for j in range(1, ncol):
        ocopy(j).start()
    total = osend[c]
    for j in range(1, ncol):
        ocopy(j).wait_recv()
    for j in range(1, ncol):
        total = total + orecv[j]
    out_ref[...] = total

    for j in range(1, ncol):
        ocopy(j).wait_send()
        for k in range(own):
            xcopy(k, j).wait_send()
    for k in range(own):
        for zz in range(nhi):
            across(k, zz).wait_send()
        for d in range(nhi):
            @pl.when(jnp.logical_and(z >= d, z < nhi - 1))
            def _():
                up(k, d).wait_send()

            @pl.when(jnp.logical_and(z + d < nhi, z > 0))
            def _():
                down(k, d).wait_send()


def body(nblk, ncol, amplitudes, integrals, block_ids, mirror):
    blocks_here, rows, width = amplitudes.shape
    _, ab, own, _ = integrals.shape
    pairs = mirror.shape[0]
    own_pairs = pairs // ncol
    padded = -(-width // 128) * 128
    nhi = nblk // 2
    f32 = jnp.float32
    dma = pltpu.SemaphoreType.DMA
    return pl.pallas_call(
        functools.partial(kernel, nblk, ncol),
        out_shape=jax.ShapeDtypeStruct((own_pairs, ab), f32),
        in_specs=[
            pl.BlockSpec(memory_space=pl.ANY),
            pl.BlockSpec(memory_space=pl.ANY),
            pl.BlockSpec(memory_space=pltpu.SMEM),
            pl.BlockSpec(memory_space=pltpu.SMEM),
        ],
        out_specs=pl.BlockSpec(memory_space=pltpu.VMEM),
        scratch_shapes=[
            pltpu.VMEM((blocks_here, rows, width), f32),
            pltpu.VMEM((own, 2 * width, ab), f32),
            pltpu.VMEM((own, padded, 2 * ab), jnp.bfloat16),
            pltpu.VMEM((own, padded, 2 * ab), jnp.bfloat16),
            pltpu.VMEM((ncol, own, rows, width), f32),
            pltpu.VMEM((ncol, own, rows, width), f32),
            pltpu.VMEM((own, nblk, rows, width), f32),
            pltpu.VMEM((2 * pairs, padded), f32),
            pltpu.VMEM((pairs, ab), f32),
            pltpu.VMEM((ncol, own_pairs, ab), f32),
            pltpu.VMEM((ncol, own_pairs, ab), f32),
            dma(()),
            dma((own,)),
            dma((ncol, own)),
            dma((ncol, own)),
            dma((own, nhi)),
            dma((own, nhi)),
            dma((own, nhi)),
            dma((own, nblk)),
            dma((ncol,)),
            dma((ncol,)),
        ],
        compiler_params=pltpu.CompilerParams(
            collective_id=0, has_side_effects=True, vmem_limit_bytes=60 * 1024 * 1024
        ),
    )(amplitudes, jnp.transpose(integrals, (2, 3, 0, 1)), block_ids, mirror)


def solution(mesh):
    in_specs = (P("col", "blk", None), P(None, "blk", "col", None), P(), P())
    out_specs = P("col", "blk")
    call = functools.partial(body, mesh.shape["blk"], mesh.shape["col"])
    return jax.shard_map(call, mesh=mesh, in_specs=in_specs, out_specs=out_specs, check_vma=False)
```

```python
import functools

import jax
import jax.numpy as jnp
from jax import lax
from jax.experimental import pallas as pl
from jax.experimental.pallas import tpu as pltpu
from jax.sharding import PartitionSpec as P

MESH = pl.DeviceIdType.MESH


def kernel(
    nblk, ncol,
    amp_hbm, int_hbm, ids, mirror, out_ref,
    amp_v, int_v, hi, lo, core_out, core_in, sendb, landed, gath, feed, swp, osend, orecv,
    amp_sem, int_sem, cs, cr, xs, xr, us, ds, ys, gr, os_, or_,
):
    blocks_here = amp_v.shape[0]
    own = int_v.shape[0]
    rows = amp_v.shape[1]
    width = amp_v.shape[2]
    ab = int_v.shape[2]
    padded = hi.shape[1]
    pairs = feed.shape[0] // 2
    own_pairs = osend.shape[1]
    nhi = nblk // 2
    half = nblk // 2
    b = lax.axis_index("blk")
    c = lax.axis_index("col")
    z = b // 2
    y = b % 2
    nx = ncol // 2
    x = c // 2
    q = c % 2
    partner = z * 2 + (1 - y)

    amp_copies = []
    for i in range(4):
        low, high = blocks_here * i // 4, blocks_here * (i + 1) // 4
        cp = pltpu.make_async_copy(
            amp_hbm.at[low:high], amp_v.at[low:high], amp_sem.at[i])
        cp.start()
        amp_copies.append(cp)
    barrier = pltpu.get_barrier_semaphore()
    for j in range(1, ncol):
        pl.semaphore_signal(barrier, inc=1, device_id=(b, (c + j) % ncol), device_id_type=MESH)
    pl.semaphore_signal(barrier, inc=1, device_id=(partner, c), device_id_type=MESH)

    @pl.when(z < nhi - 1)
    def _():
        pl.semaphore_signal(barrier, inc=1, device_id=(b + 2, c), device_id_type=MESH)

    @pl.when(z > 0)
    def _():
        pl.semaphore_signal(barrier, inc=1, device_id=(b - 2, c), device_id_type=MESH)

    ends = (z == 0).astype(jnp.int32) + (z == nhi - 1).astype(jnp.int32)
    pl.semaphore_wait(barrier, ncol + 2 - ends)

    def core_copy(k, i):
        return pltpu.make_async_remote_copy(
            src_ref=core_out.at[i, k], dst_ref=core_in.at[i, k],
            send_sem=cs.at[i, k], recv_sem=cr.at[i, k],
            device_id=(b, x * 2 + 1 - q), device_id_type=MESH)

    def xcopy(k, i):
        return pltpu.make_async_remote_copy(
            src_ref=sendb.at[i, k], dst_ref=landed.at[i, k],
            send_sem=xs.at[i, k], recv_sem=xr.at[i, k],
            device_id=(b, (x + i) % nx * 2 + q), device_id_type=MESH)

    def gcopy(k, src, sem, target):
        return pltpu.make_async_remote_copy(
            src_ref=gath.at[k, src], dst_ref=gath.at[k, src],
            send_sem=sem, recv_sem=gr.at[k, src],
            device_id=(target, c), device_id_type=MESH)

    def up(k, d):
        return gcopy(k, b - 2 * d, us.at[k, d], b + 2)

    def down(k, d):
        return gcopy(k, b + 2 * d, ds.at[k, d], b - 2)

    def across(k, zz):
        return gcopy(k, zz * 2 + y, ys.at[k, zz], partner)

    def arrived(k, src):
        gcopy(k, src, us.at[k, 0], partner).wait_recv()

    base = c * blocks_here

    def wanted(k, dest):
        here = ids[dest * own + k] - base
        ok = jnp.logical_and(here >= 0, here < blocks_here)
        at = jnp.minimum(jnp.maximum(here, 0), blocks_here - 1)
        return jnp.where(ok, amp_v[at], 0.0)

    for cp in amp_copies:
        cp.wait()
    int_copies = {}
    for k in range(own):
        cp = pltpu.make_async_copy(int_hbm.at[k], int_v.at[k].reshape(width, 2, ab), int_sem.at[k])
        cp.start()
        int_copies[k] = cp

    for k in range(own):
        for i in [*range(1, nx), 0]:
            core_out[i, k] = wanted(k, (x + i) % nx * 2 + 1 - q)
            core_copy(k, i).start()
    for k in range(own):
        for i in range(1, nx):
            mine = wanted(k, (x + i) % nx * 2 + q)
            core_copy(k, i).wait_recv()
            sendb[i, k] = mine + core_in[i, k]
            xcopy(k, i).start()

    tail = (width // 128) * 128
    if padded > width:
        feed[:, tail:] = jnp.zeros((2 * pairs, padded - tail), jnp.float32)

    def convert(k):
        int_copies[k].wait()
        whole = width // 16

        def split(at, count):
            for w in range(2):
                v = int_v[k, pl.ds(at * 2 + w, count, stride=2), :]
                h = v.astype(jnp.bfloat16)
                l = (v - h.astype(jnp.float32)).astype(jnp.bfloat16)
                if count < 16:
                    blank = jnp.zeros((16 - count, ab), jnp.bfloat16)
                    h = jnp.concatenate([h, blank], axis=0)
                    l = jnp.concatenate([l, blank], axis=0)
                hi[k, pl.ds(at, 16), w * ab:(w + 1) * ab] = h
                lo[k, pl.ds(at, 16), w * ab:(w + 1) * ab] = l

        def strip(i, carry):
            split(pl.multiple_of(i * 16, 16), 16)
            return carry

        lax.fori_loop(0, whole, strip, 0, unroll=4)
        end = whole * 16
        if width > end:
            split(end, width - end)
            end += 16
        if padded > end:
            hi[k, end:] = jnp.zeros((padded - end, 2 * ab), jnp.bfloat16)
            lo[k, end:] = jnp.zeros((padded - end, 2 * ab), jnp.bfloat16)

    def own_piece(k):
        total = wanted(k, c)
        core_copy(k, 0).wait_recv()
        total = total + core_in[0, k]
        for i in range(1, nx):
            xcopy(k, i).wait_recv()
            total = total + landed[i, k]
        gath[k, b] = total
        across(k, z).start()

        @pl.when(z < nhi - 1)
        def _():
            up(k, 0).start()

        @pl.when(z > 0)
        def _():
            down(k, 0).start()

    def relay(k, d):
        @pl.when(z >= d)
        def _():
            arrived(k, b - 2 * d)

            @pl.when(z < nhi - 1)
            def _():
                up(k, d).start()

            across(k, z - d).start()

        @pl.when(z + d < nhi)
        def _():
            arrived(k, b + 2 * d)

            @pl.when(z > 0)
            def _():
                down(k, d).start()

            across(k, z + d).start()

    def multiply(k, acc):
        for zz in range(nhi):
            arrived(k, zz * 2 + 1 - y)
        for i in range(half):
            first = gath[k, i]
            second = gath[k, half + i]
            feed[i * rows:(i + 1) * rows, :width] = first + second
            feed[pairs + i * rows:pairs + (i + 1) * rows, :width] = first - second
        f = feed[...]
        fh = f.astype(jnp.bfloat16)
        fl = (f - fh.astype(jnp.float32)).astype(jnp.bfloat16)
        both = jnp.concatenate([fh, fl], axis=0)
        big = jnp.dot(both, hi[k], preferred_element_type=jnp.float32)
        small = jnp.dot(fh, lo[k], preferred_element_type=jnp.float32)
        part = big[:2 * pairs] + (big[2 * pairs:] + small)
        new = [part[:pairs, :ab], part[pairs:, ab:]]
        return new if acc is None else [u + v for u, v in zip(acc, new)]

    events = sorted((k * 1 + d * 100, d, k) for k in range(own) for d in range(nhi))
    convert(0)
    ready = 1
    for _, d, k in events:
        if d == 0:
            own_piece(k)
        else:
            relay(k, d)
        if ready < own:
            convert(ready)
            ready += 1
    acc = None
    for k in range(own):
        acc = multiply(k, acc)

    x_part, y_part = acc
    swp[...] = 0.5 * (x_part - y_part)
    direct = 0.5 * (x_part + y_part)
    for g in range(ncol):
        for i in range(own_pairs):
            p = g * own_pairs + i
            osend[g, i:i + 1, :] = direct[p:p + 1] + swp[pl.ds(mirror[p], 1), :]

    def ocopy(j):
        dest = (c + j) % ncol
        return pltpu.make_async_remote_copy(
            src_ref=osend.at[dest], dst_ref=orecv.at[j],
            send_sem=os_.at[j], recv_sem=or_.at[j],
            device_id=(b, dest), device_id_type=MESH)

    for j in range(1, ncol):
        ocopy(j).start()
    total = osend[c]
    for j in range(1, ncol):
        ocopy(j).wait_recv()
    for j in range(1, ncol):
        total = total + orecv[j]
    out_ref[...] = total

    for j in range(1, ncol):
        ocopy(j).wait_send()
    for k in range(own):
        for i in range(nx):
            core_copy(k, i).wait_send()
        for i in range(1, nx):
            xcopy(k, i).wait_send()
        for zz in range(nhi):
            across(k, zz).wait_send()
        for d in range(nhi):
            @pl.when(jnp.logical_and(z >= d, z < nhi - 1))
            def _():
                up(k, d).wait_send()

            @pl.when(jnp.logical_and(z + d < nhi, z > 0))
            def _():
                down(k, d).wait_send()


def body(nblk, ncol, amplitudes, integrals, block_ids, mirror):
    blocks_here, rows, width = amplitudes.shape
    _, ab, own, _ = integrals.shape
    pairs = mirror.shape[0]
    own_pairs = pairs // ncol
    padded = -(-width // 128) * 128
    nhi = nblk // 2
    nx = ncol // 2
    f32 = jnp.float32
    dma = pltpu.SemaphoreType.DMA
    return pl.pallas_call(
        functools.partial(kernel, nblk, ncol),
        out_shape=jax.ShapeDtypeStruct((own_pairs, ab), f32),
        in_specs=[
            pl.BlockSpec(memory_space=pl.ANY),
            pl.BlockSpec(memory_space=pl.ANY),
            pl.BlockSpec(memory_space=pltpu.SMEM),
            pl.BlockSpec(memory_space=pltpu.SMEM),
        ],
        out_specs=pl.BlockSpec(memory_space=pltpu.VMEM),
        scratch_shapes=[
            pltpu.VMEM((blocks_here, rows, width), f32),
            pltpu.VMEM((own, 2 * width, ab), f32),
            pltpu.VMEM((own, padded, 2 * ab), jnp.bfloat16),
            pltpu.VMEM((own, padded, 2 * ab), jnp.bfloat16),
            pltpu.VMEM((nx, own, rows, width), f32),
            pltpu.VMEM((nx, own, rows, width), f32),
            pltpu.VMEM((nx, own, rows, width), f32),
            pltpu.VMEM((nx, own, rows, width), f32),
            pltpu.VMEM((own, nblk, rows, width), f32),
            pltpu.VMEM((2 * pairs, padded), f32),
            pltpu.VMEM((pairs, ab), f32),
            pltpu.VMEM((ncol, own_pairs, ab), f32),
            pltpu.VMEM((ncol, own_pairs, ab), f32),
            dma((4,)),
            dma((own,)),
            dma((nx, own)),
            dma((nx, own)),
            dma((nx, own)),
            dma((nx, own)),
            dma((own, nhi)),
            dma((own, nhi)),
            dma((own, nhi)),
            dma((own, nblk)),
            dma((ncol,)),
            dma((ncol,)),
        ],
        compiler_params=pltpu.CompilerParams(
            collective_id=0, has_side_effects=True, vmem_limit_bytes=60 * 1024 * 1024
        ),
    )(amplitudes, jnp.transpose(integrals, (2, 3, 0, 1)), block_ids, mirror)


def solution(mesh):
    in_specs = (P("col", "blk", None), P(None, "blk", "col", None), P(), P())
    out_specs = P("col", "blk")
    call = functools.partial(body, mesh.shape["blk"], mesh.shape["col"])
    return jax.shard_map(call, mesh=mesh, in_specs=in_specs, out_specs=out_specs, check_vma=False)
```
